128 devices in a mesh: ctx: 16 (over x, z_hi, core), tp: 8 (over y, z_lo).
Axes of the slice: x: 4, y: 4, z: 4 (z_hi: 2, z_lo: 2; z = z_hi * 2 + z_lo), core: 2. Of those that a mesh axis runs over, the one named last changes fastest.
Arguments:
- query_proj: bfloat16 [6144, 4096], P('ctx', 'tp'), may hold values from -6 to 6
- key_proj: bfloat16 [6144, 4096], P('ctx', 'tp'), may hold values from -6 to 6
- value_proj: bfloat16 [6144, 4096], P('ctx', 'tp'), may hold values from -6 to 6
- saved_conv: bfloat16 [6144, 4096], P('ctx', 'tp'), may hold values from -6 to 6
- grad_out: bfloat16 [6144, 4096], P(('ctx', 'tp')), may hold values from -6 to 6
- filters: bfloat16 [256, 6144], P('tp'), may hold values from -0.109375 to 0.109375
- featurizer: float32 [3, 3, 4096], P(None, None, 'tp'), may hold values from -2 to 2
Outputs:
- grad_query: bfloat16 [6144, 4096], P('ctx', 'tp')
- grad_key: bfloat16 [6144, 4096], P('ctx', 'tp')
- grad_value: bfloat16 [6144, 4096], P('ctx', 'tp')
The draws below stay inside these ranges and needn't reach their ends.
All inputs are finite; a program needn't handle non-finite values.
Results may differ from the reference program's by a relative error of at most 0.012.
Values may be sent and summed in bfloat16 or wider, within the bound.
A program may use at most 256 MiB of HBM per device.

```python
import jax
import jax.numpy as jnp

CHAN = 4096
GSIZE = 16
TAPS = 3
GROUPS = 256
TOKENS = 6144


def levels(key, extent, cuts, least, high):
    level, own = 1.0, jax.random.fold_in(key, 6)
    for dim, parts in cuts:
        draws = jnp.exp(jax.random.uniform(jax.random.fold_in(own, dim), (parts,), jnp.float32, least / len(cuts), high / len(cuts)))
        level = level * jnp.repeat(draws, extent[dim] // parts).reshape([-1 if axis == dim else 1 for axis in range(len(extent))])
    return level


def scatter_about(rng, extent, deviation, reach, cuts=(), dtype=jnp.bfloat16):
    level = levels(rng, extent, cuts, -0.22, 0.18) if cuts else 1.0
    result = jax.random.normal(rng, extent, jnp.float32) * deviation * level
    return jnp.minimum(jnp.maximum(result, -reach), reach).astype(dtype)


def setup_inputs(seed: int = 0) -> dict:
    seeds = jax.random.split(jax.random.key(seed), 8)
    return {
        "query_proj": scatter_about(seeds[0], (TOKENS, CHAN), 1.0, 6.0, ((0, 16), (1, 8))),
        "key_proj": scatter_about(seeds[1], (TOKENS, CHAN), 1.0, 6.0, ((0, 16), (1, 8))),
        "value_proj": scatter_about(seeds[2], (TOKENS, CHAN), 1.0, 6.0, ((0, 16), (1, 8))),
        "saved_conv": scatter_about(seeds[3], (TOKENS, CHAN), 1.0, 6.0, ((0, 16), (1, 8))),
        "grad_out": scatter_about(seeds[4], (TOKENS, CHAN), 1.0, 6.0, ((0, 128),)),
        "filters": scatter_about(seeds[5], (GROUPS, TOKENS), (TOKENS // 2) ** -0.5, 0.109375, ((0, 8),)),
        "featurizer": scatter_about(seeds[6], (3, TAPS, CHAN), 0.4, 2.0, ((2, 8),), jnp.float32),
    }


def featurize(stream, kernel):
    length = stream.shape[0]
    padded = jnp.pad(stream, ((TAPS - 1, 0), (0, 0)))
    total = kernel[0] * padded[TAPS - 1:TAPS - 1 + length]
    for offset in range(1, TAPS):
        total = total + kernel[offset] * padded[TAPS - 1 - offset:TAPS - 1 - offset + length]
    return total


def spread(stream, kernel):
    length = stream.shape[0]
    padded = jnp.pad(stream, ((0, TAPS - 1), (0, 0)))
    total = kernel[0] * padded[0:length]
    for offset in range(1, TAPS):
        total = total + kernel[offset] * padded[offset:offset + length]
    return total


def reference(query_proj, key_proj, value_proj, saved_conv, grad_out, filters, featurizer):
    query_feat = featurize(query_proj.astype(jnp.float32), featurizer[0])
    key_feat = featurize(key_proj.astype(jnp.float32), featurizer[1])
    value_feat = featurize(value_proj.astype(jnp.float32), featurizer[2])
    upstream = grad_out.astype(jnp.float32)
    grad_qfeat = upstream * saved_conv.astype(jnp.float32)
    grad_conv = (upstream * query_feat).astype(jnp.bfloat16)
    reversed_grad = grad_conv.astype(jnp.float32)[::-1]
    per_channel = jnp.repeat(filters.astype(jnp.float32), GSIZE, axis=0).T
    length = 2 * TOKENS
    spectrum = jnp.fft.rfft(reversed_grad, n=length, axis=0) * jnp.fft.rfft(per_channel, n=length, axis=0)
    grad_mix = jnp.fft.irfft(spectrum, n=length, axis=0)[:TOKENS][::-1].astype(jnp.float32)
    grad_kfeat = grad_mix * value_feat
    grad_vfeat = grad_mix * key_feat
    grad_query = spread(grad_qfeat, featurizer[0]).astype(jnp.bfloat16)
    grad_key = spread(grad_kfeat, featurizer[1]).astype(jnp.bfloat16)
    grad_value = spread(grad_vfeat, featurizer[2]).astype(jnp.bfloat16)
    return (grad_query, grad_key, grad_value)
```

```python
import jax
import jax.numpy as jnp
from jax import lax
from jax.experimental import pallas as pl
from jax.experimental.pallas import tpu as pltpu
from jax.sharding import PartitionSpec as P

GSIZE = 16
TAPS = 3
LANE = 128
HALO = 8
BLOCK = 256
MESH = pl.DeviceIdType.MESH


def kernel(
    n_ctx,
    n_tp,
    q_hbm,
    k_hbm,
    v_hbm,
    sc_hbm,
    go_hbm,
    filt_hbm,
    taps,
    oq_hbm,
    ok_hbm,
    ov_hbm,
    q_v,
    k_v,
    v_v,
    sc_v,
    go_v,
    filt_v,
    prev_v,
    next_v,
    join,
    qfeat,
    kfeat,
    vfeat,
    gq,
    toep,
    gct,
    land,
    xrows,
    acc,
    back,
    mix,
    prod,
    oq_v,
    ok_v,
    ov_v,
    local_sem,
    tp_send,
    tp_recv,
    halo_send,
    halo_recv,
    fwd_send,
    fwd_recv,
    bwd_send,
    bwd_recv,
    out_sem,
):
    me = lax.axis_index("ctx")
    mytp = lax.axis_index("tp")
    rows, channels = q_v.shape
    own_rows = go_hbm.shape[0]
    tokens = filt_v.shape[1]
    half_ch = channels // 2
    blocks = channels // LANE
    tiles = rows // LANE
    up = lax.rem(me + 1, n_ctx)
    down = lax.rem(me + n_ctx - 1, n_ctx)

    loads = []
    for index, (src, dst) in enumerate(
        ((q_hbm, q_v), (filt_hbm, filt_v), (k_hbm, k_v), (v_hbm, v_v), (sc_hbm, sc_v))
    ):
        copy = pltpu.make_async_copy(src, dst, local_sem.at[index])
        copy.start()
        loads.append(copy)
    own_go = pltpu.make_async_copy(
        go_hbm.at[:, pl.ds(pl.multiple_of(mytp * channels, channels), channels)],
        go_v.at[pl.ds(pl.multiple_of(mytp * own_rows, own_rows), own_rows), :],
        local_sem.at[5],
    )
    own_go.start()

    barrier = pltpu.get_barrier_semaphore()
    for step in range(1, n_tp):
        pl.semaphore_signal(
            barrier, inc=1, device_id={"tp": lax.rem(mytp + step, n_tp)}, device_id_type=MESH
        )
    for step in range(1, n_ctx):
        pl.semaphore_signal(
            barrier, inc=1, device_id={"ctx": lax.rem(me + step, n_ctx)}, device_id_type=MESH
        )
    pl.semaphore_wait(barrier, n_tp + n_ctx - 2)

    tp_copies = []
    for step in range(1, n_tp):
        peer = lax.rem(mytp + step, n_tp)
        copy = pltpu.make_async_remote_copy(
            src_ref=go_hbm.at[:, pl.ds(pl.multiple_of(peer * channels, channels), channels)],
            dst_ref=go_v.at[pl.ds(pl.multiple_of(mytp * own_rows, own_rows), own_rows), :],
            send_sem=tp_send.at[step],
            recv_sem=tp_recv.at[step],
            device_id={"tp": peer},
            device_id_type=MESH,
        )
        copy.start()
        tp_copies.append(copy)

    halo_copies = []
    for index, src in enumerate((q_hbm, k_hbm, v_hbm)):
        copy = pltpu.make_async_remote_copy(
            src_ref=src.at[pl.ds(rows - HALO, HALO), :],
            dst_ref=prev_v.at[index],
            send_sem=halo_send.at[index],
            recv_sem=halo_recv.at[index],
            device_id={"ctx": up},
            device_id_type=MESH,
        )
        copy.start()
        halo_copies.append(copy)
    for index, src in enumerate((k_hbm, v_hbm)):
        copy = pltpu.make_async_remote_copy(
            src_ref=src.at[pl.ds(0, HALO), :],
            dst_ref=next_v.at[index],
            send_sem=halo_send.at[3 + index],
            recv_sem=halo_recv.at[3 + index],
            device_id={"ctx": down},
            device_id_type=MESH,
        )
        copy.start()
        halo_copies.append(copy)

    loads[1].wait()
    n_groups = filt_v.shape[0]
    flip = (
        lax.broadcasted_iota(jnp.int32, (LANE, LANE), 0)
        + lax.broadcasted_iota(jnp.int32, (LANE, LANE), 1)
        == LANE - 1
    ).astype(jnp.float32).astype(jnp.bfloat16)
    lag_tiles = tokens // LANE
    for half in range(2):
        pick = (
            lax.broadcasted_iota(jnp.int32, (16, n_groups), 1) == me + half * n_ctx
        ).astype(jnp.float32).astype(jnp.bfloat16)
        line = jnp.dot(pick, filt_v[...], preferred_element_type=jnp.float32)
        line = line.astype(jnp.bfloat16)
        stack = jnp.concatenate(
            [line[:, LANE * t : LANE * (t + 1)] for t in range(lag_tiles - 1, -1, -1)], axis=0
        )
        turned = jnp.dot(stack, flip, preferred_element_type=jnp.float32)
        turned = jnp.concatenate(
            [turned[16 * t : 16 * t + 8] for t in range(lag_tiles)]
            + [jnp.zeros((8, 2 * LANE), jnp.float32)],
            axis=1,
        )
        base = pltpu.roll(turned, 1, 1, stride=1, stride_axis=0)
        for part in range(LANE // 16):
            toep[half, 16 * part : 16 * (part + 1), :] = jnp.concatenate(
                [
                    base if part == 0 else pltpu.roll(base, 16 * part, 1),
                    pltpu.roll(base, 16 * part + 8, 1),
                ],
                axis=0,
            ).astype(jnp.bfloat16)

    def columns(block):
        return slice(LANE * block, LANE * (block + 1))

    def feature(stream, current, block, following, count):
        before = prev_v[stream, :, columns(block)].astype(jnp.float32)
        join[0:HALO] = jnp.where(me == 0, 0.0, before)
        join[HALO : HALO + rows] = current[:, columns(block)].astype(jnp.float32)
        if following is not None:
            join[HALO + rows : 2 * HALO + rows] = next_v[following, :, columns(block)].astype(
                jnp.float32
            )
        total = taps[stream, 0:1, columns(block)] * join[HALO : HALO + count]
        for offset in range(1, TAPS):
            total = total + taps[stream, offset : offset + 1, columns(block)] * (
                join[HALO - offset : HALO - offset + count]
            )
        return total

    loads[0].wait()
    halo_copies[0].wait()
    for block in range(blocks):
        qfeat[block] = feature(0, q_v, block, None, rows)

    own_go.wait()
    for copy in tp_copies:
        copy.wait()
    fwd_copies = [[], []]
    for half in range(2):
        for block in range(half * blocks // 2, (half + 1) * blocks // 2):
            conv = go_v[:, columns(block)].astype(jnp.float32) * qfeat[block]
            gct[columns(block), :] = conv.T.astype(jnp.bfloat16)
        for step in range(1, n_ctx):
            peer = lax.rem(me + step, n_ctx)
            copy = pltpu.make_async_remote_copy(
                src_ref=gct.at[pl.ds(pl.multiple_of(half * half_ch + peer * GSIZE, GSIZE), GSIZE), :],
                dst_ref=land.at[half, me],
                send_sem=fwd_send.at[half, step],
                recv_sem=fwd_recv.at[half, step],
                device_id={"ctx": peer},
                device_id_type=MESH,
            )
            copy.start()
            fwd_copies[half].append(copy)
        land[half, me] = gct[
            pl.ds(pl.multiple_of(half * half_ch + me * GSIZE, GSIZE), GSIZE), :
        ]

    loads[4].wait()
    for block in range(blocks):
        gq[block, 0:rows] = go_v[:, columns(block)].astype(jnp.float32) * sc_v[
            :, columns(block)
        ].astype(jnp.float32)
    gq_copy = pltpu.make_async_remote_copy(
        src_ref=gq.at[:, pl.ds(0, HALO), :],
        dst_ref=gq.at[:, pl.ds(rows, HALO), :],
        send_sem=halo_send.at[5],
        recv_sem=halo_recv.at[5],
        device_id={"ctx": down},
        device_id_type=MESH,
    )
    gq_copy.start()
    loads[2].wait()
    loads[3].wait()
    for copy in halo_copies[1:]:
        copy.wait()
    for block in range(blocks):
        kfeat[block] = feature(1, k_v, block, 0, rows + HALO)
        vfeat[block] = feature(2, v_v, block, 1, rows + HALO)

    bwd_copies = [[], []]
    row_blocks = tokens // BLOCK
    for half in range(2):
        xrows[row_blocks * GSIZE :] = jnp.zeros(
            (xrows.shape[0] - row_blocks * GSIZE, BLOCK), jnp.bfloat16
        )
        for copy in fwd_copies[half]:
            copy.wait()
        for source in range(n_ctx):
            for tile in range(tiles):
                place, side = divmod(source * tiles + tile, 2)
                xrows[GSIZE * place : GSIZE * (place + 1), columns(side)] = land[
                    half, source, :, columns(tile)
                ]
        for part in range(3):
            amount = row_blocks * GSIZE - part * LANE
            left = jnp.concatenate(
                [xrows[GSIZE * d : GSIZE * d + amount, :] for d in range(8 * part, 8 * part + 8)],
                axis=1,
            )
            right = jnp.concatenate(
                [
                    toep[half, :, LANE * (lag_tiles - e) : LANE * (lag_tiles - e + 2)]
                    for e in range(16 * part, 16 * part + 16)
                ],
                axis=0,
            )
            product = jnp.dot(left, right, preferred_element_type=jnp.float32)
            if part == 0:
                acc[...] = product
            else:
                acc[0:amount] += product
        for target in range(n_ctx):
            for tile in range(tiles + 1):
                place, side = divmod(target * tiles + tile, 2)
                if place < row_blocks:
                    value = acc[GSIZE * place : GSIZE * (place + 1), columns(side)]
                else:
                    value = jnp.zeros((GSIZE, LANE), jnp.float32)
                back[half, target, :, columns(tile)] = value.astype(jnp.bfloat16)
        spot = pl.ds(pl.multiple_of(half * half_ch + me * GSIZE, GSIZE), GSIZE)
        for step in range(1, n_ctx):
            peer = lax.rem(me + step, n_ctx)
            copy = pltpu.make_async_remote_copy(
                src_ref=back.at[half, peer],
                dst_ref=mix.at[spot, :],
                send_sem=bwd_send.at[half, step],
                recv_sem=bwd_recv.at[half, step],
                device_id={"ctx": peer},
                device_id_type=MESH,
            )
            copy.start()
            bwd_copies[half].append(copy)
        mix[spot, :] = back[half, me]

    def spread(stream, load, block):
        total = taps[stream, 0:1, columns(block)] * load(0)
        for offset in range(1, TAPS):
            total = total + taps[stream, offset : offset + 1, columns(block)] * load(offset)
        return total.astype(jnp.bfloat16)

    gq_copy.wait()
    outs = []
    for block in range(blocks):
        gq[block, rows : rows + HALO] = jnp.where(
            me == n_ctx - 1, 0.0, gq[block, rows : rows + HALO]
        )
        oq_v[:, columns(block)] = spread(
            0, lambda offset: gq[block, offset : offset + rows], block
        )
    copy = pltpu.make_async_copy(oq_v, oq_hbm, out_sem.at[0])
    copy.start()
    outs.append(copy)

    for half in range(2):
        for copy in bwd_copies[half]:
            copy.wait()
        for block in range(half * blocks // 2, (half + 1) * blocks // 2):
            here = mix[columns(block), 0:rows].astype(jnp.float32).T
            there = mix[columns(block), rows : rows + LANE].astype(jnp.float32).T
            whole = jnp.concatenate([here, there[0:HALO]], axis=0)
            prod[0] = whole * vfeat[block]
            prod[1] = whole * kfeat[block]
            ok_v[:, columns(block)] = spread(
                1, lambda offset: prod[0, offset : offset + rows], block
            )
            ov_v[:, columns(block)] = spread(
                2, lambda offset: prod[1, offset : offset + rows], block
            )
        part = pl.ds(half * half_ch, half_ch)
        for index, (src, dst) in enumerate(((ok_v, ok_hbm), (ov_v, ov_hbm))):
            copy = pltpu.make_async_copy(
                src.at[:, part], dst.at[:, part], out_sem.at[1 + 2 * half + index]
            )
            copy.start()
            outs.append(copy)
    for copy in outs:
        copy.wait()


def body(n_ctx, n_tp, query_proj, key_proj, value_proj, saved_conv, grad_out, filters, featurizer):
    rows, channels = query_proj.shape
    tokens = filters.shape[1]
    blocks = channels // LANE
    bf16, f32 = jnp.bfloat16, jnp.float32
    dma = pltpu.SemaphoreType.DMA
    hbm = pl.BlockSpec(memory_space=pl.ANY)
    stream = pltpu.VMEM((rows, channels), bf16)
    conv_rows = tokens // BLOCK * GSIZE
    run = pl.pallas_call(
        lambda *refs: kernel(n_ctx, n_tp, *refs),
        out_shape=[jax.ShapeDtypeStruct((rows, channels), bf16)] * 3,
        in_specs=[hbm] * 6 + [pl.BlockSpec(memory_space=pltpu.VMEM)],
        out_specs=[hbm] * 3,
        scratch_shapes=[
            stream,
            stream,
            stream,
            stream,
            stream,
            pltpu.VMEM(filters.shape, bf16),
            pltpu.VMEM((3, HALO, channels), bf16),
            pltpu.VMEM((2, HALO, channels), bf16),
            pltpu.VMEM((rows + 2 * HALO, LANE), f32),
            pltpu.VMEM((blocks, rows, LANE), f32),
            pltpu.VMEM((blocks, rows + HALO, LANE), f32),
            pltpu.VMEM((blocks, rows + HALO, LANE), f32),
            pltpu.VMEM((blocks, rows + HALO, LANE), f32),
            pltpu.VMEM((2, LANE, tokens + 2 * LANE), bf16),
            pltpu.VMEM((channels, rows), bf16),
            pltpu.VMEM((2, n_ctx, GSIZE, rows), bf16),
            pltpu.VMEM((conv_rows + LANE, BLOCK), bf16),
            pltpu.VMEM((conv_rows, BLOCK), f32),
            pltpu.VMEM((2, n_ctx, GSIZE, rows + LANE), bf16),
            pltpu.VMEM((channels, rows + LANE), bf16),
            pltpu.VMEM((2, rows + HALO, LANE), f32),
            stream,
            stream,
            stream,
            dma((6,)),
            dma((n_tp,)),
            dma((n_tp,)),
            dma((6,)),
            dma((6,)),
            dma((2, n_ctx)),
            dma((2, n_ctx)),
            dma((2, n_ctx)),
            dma((2, n_ctx)),
            dma((5,)),
        ],
        compiler_params=pltpu.CompilerParams(collective_id=0, has_side_effects=True),
    )
    return tuple(
        run(query_proj, key_proj, value_proj, saved_conv, grad_out, filters, featurizer)
    )


def solution(mesh):
    n_ctx, n_tp = mesh.shape["ctx"], mesh.shape["tp"]
    return jax.shard_map(
        lambda *args: body(n_ctx, n_tp, *args),
        mesh=mesh,
        in_specs=(
            P("ctx", "tp"),
            P("ctx", "tp"),
            P("ctx", "tp"),
            P("ctx", "tp"),
            P(("ctx", "tp"), None),
            P("tp", None),
            P(None, None, "tp"),
        ),
        out_specs=(P("ctx", "tp"), P("ctx", "tp"), P("ctx", "tp")),
        check_vma=False,
    )
```

```python
import jax
import jax.numpy as jnp
from jax import lax
from jax.experimental import pallas as pl
from jax.experimental.pallas import tpu as pltpu
from jax.sharding import PartitionSpec as P

GSIZE = 16
TAPS = 3
LANE = 128
HALO = 8
BLOCK = 256
MESH = pl.DeviceIdType.MESH


def kernel(
    n_ctx,
    n_tp,
    q_hbm,
    k_hbm,
    v_hbm,
    sc_hbm,
    go_hbm,
    filt_hbm,
    taps_hbm,
    taps,
    oq_v,
    ok_v,
    ov_v,
    mix,
    kfeat,
    vfeat,
    q_v,
    k_v,
    v_v,
    sc_v,
    go_v,
    filt_v,
    prev_v,
    next_v,
    join,
    qfeat,
    gq,
    toep,
    gct,
    land,
    xrows,
    acc,
    back,
    prod,
    local_sem,
    tp_send,
    tp_recv,
    halo_send,
    halo_recv,
    fwd_send,
    fwd_recv,
    bwd_send,
    bwd_recv,
):
    me = lax.axis_index("ctx")
    mytp = lax.axis_index("tp")
    rows, channels = q_v.shape
    own_rows = go_hbm.shape[0]
    tokens = filt_v.shape[1]
    half_ch = channels // 2
    blocks = channels // LANE
    tiles = rows // LANE
    up = lax.rem(me + 1, n_ctx)
    down = lax.rem(me + n_ctx - 1, n_ctx)

    loads = []
    for index, (src, dst) in enumerate(
        (
            (q_hbm, q_v),
            (filt_hbm, filt_v),
            (k_hbm, k_v),
            (v_hbm, v_v),
            (sc_hbm, sc_v),
            (taps_hbm, taps),
        )
    ):
        copy = pltpu.make_async_copy(src, dst, local_sem.at[index])
        copy.start()
        loads.append(copy)
    own_go = pltpu.make_async_copy(
        go_hbm.at[:, pl.ds(pl.multiple_of(mytp * channels, channels), channels)],
        go_v.at[pl.ds(pl.multiple_of(mytp * own_rows, own_rows), own_rows), :],
        local_sem.at[6],
    )
    own_go.start()

    barrier = pltpu.get_barrier_semaphore()
    for step in range(1, n_tp):
        pl.semaphore_signal(
            barrier, inc=1, device_id={"tp": lax.rem(mytp + step, n_tp)}, device_id_type=MESH
        )
    for step in range(1, n_ctx):
        pl.semaphore_signal(
            barrier, inc=1, device_id={"ctx": lax.rem(me + step, n_ctx)}, device_id_type=MESH
        )
    pl.semaphore_wait(barrier, n_tp + n_ctx - 2)

    tp_copies = [[], []]
    for half in range(2):
        for step in range(1, n_tp):
            peer = lax.rem(mytp + step, n_tp)
            source = pl.multiple_of(peer * channels + half * half_ch, half_ch)
            copy = pltpu.make_async_remote_copy(
                src_ref=go_hbm.at[:, pl.ds(source, half_ch)],
                dst_ref=go_v.at[
                    pl.ds(pl.multiple_of(mytp * own_rows, own_rows), own_rows),
                    pl.ds(half * half_ch, half_ch),
                ],
                send_sem=tp_send.at[half, step],
                recv_sem=tp_recv.at[half, step],
                device_id={"tp": peer},
                device_id_type=MESH,
            )
            copy.start()
            tp_copies[half].append(copy)

    halo_copies = []
    for index, src in enumerate((q_hbm, k_hbm, v_hbm)):
        copy = pltpu.make_async_remote_copy(
            src_ref=src.at[pl.ds(rows - HALO, HALO), :],
            dst_ref=prev_v.at[index],
            send_sem=halo_send.at[index],
            recv_sem=halo_recv.at[index],
            device_id={"ctx": up},
            device_id_type=MESH,
        )
        copy.start()
        halo_copies.append(copy)
    for index, src in enumerate((k_hbm, v_hbm)):
        copy = pltpu.make_async_remote_copy(
            src_ref=src.at[pl.ds(0, HALO), :],
            dst_ref=next_v.at[index],
            send_sem=halo_send.at[3 + index],
            recv_sem=halo_recv.at[3 + index],
            device_id={"ctx": down},
            device_id_type=MESH,
        )
        copy.start()
        halo_copies.append(copy)

    loads[1].wait()
    n_groups = filt_v.shape[0]
    flip = (
        lax.broadcasted_iota(jnp.int32, (LANE, LANE), 0)
        + lax.broadcasted_iota(jnp.int32, (LANE, LANE), 1)
        == LANE - 1
    ).astype(jnp.float32).astype(jnp.bfloat16)
    lag_tiles = tokens // LANE
    for half in range(2):
        pick = (
            lax.broadcasted_iota(jnp.int32, (16, n_groups), 1) == me + half * n_ctx
        ).astype(jnp.float32).astype(jnp.bfloat16)
        line = jnp.dot(pick, filt_v[...], preferred_element_type=jnp.float32)
        line = line.astype(jnp.bfloat16)
        stack = jnp.concatenate(
            [line[:, LANE * t : LANE * (t + 1)] for t in range(lag_tiles - 1, -1, -1)], axis=0
        )
        turned = jnp.dot(stack, flip, preferred_element_type=jnp.float32)
        turned = jnp.concatenate(
            [turned[16 * t : 16 * t + 8] for t in range(lag_tiles)]
            + [jnp.zeros((8, 2 * LANE), jnp.float32)],
            axis=1,
        )
        base = pltpu.roll(turned, 1, 1, stride=1, stride_axis=0)
        for part in range(LANE // 16):
            toep[half, 16 * part : 16 * (part + 1), :] = jnp.concatenate(
                [
                    base if part == 0 else pltpu.roll(base, 16 * part, 1),
                    pltpu.roll(base, 16 * part + 8, 1),
                ],
                axis=0,
            ).astype(jnp.bfloat16)

    def columns(block):
        return slice(LANE * block, LANE * (block + 1))

    def feature(stream, current, block, following, count):
        before = prev_v[stream, :, columns(block)].astype(jnp.float32)
        join[0:HALO] = jnp.where(me == 0, 0.0, before)
        join[HALO : HALO + rows] = current[:, columns(block)].astype(jnp.float32)
        if following is not None:
            join[HALO + rows : 2 * HALO + rows] = next_v[following, :, columns(block)].astype(
                jnp.float32
            )
        total = taps[stream, 0:1, columns(block)] * join[HALO : HALO + count]
        for offset in range(1, TAPS):
            total = total + taps[stream, offset : offset + 1, columns(block)] * (
                join[HALO - offset : HALO - offset + count]
            )
        return total

    loads[0].wait()
    loads[5].wait()
    halo_copies[0].wait()
    for block in range(blocks):
        qfeat[block] = feature(0, q_v, block, None, rows)

    own_go.wait()
    fwd_copies = [[], []]
    for half in range(2):
        for copy in tp_copies[half]:
            copy.wait()
        for block in range(half * blocks // 2, (half + 1) * blocks // 2):
            conv = go_v[:, columns(block)].astype(jnp.float32) * qfeat[block]
            gct[columns(block), :] = conv.T.astype(jnp.bfloat16)
        for step in range(1, n_ctx):
            peer = lax.rem(me + step, n_ctx)
            copy = pltpu.make_async_remote_copy(
                src_ref=gct.at[pl.ds(pl.multiple_of(half * half_ch + peer * GSIZE, GSIZE), GSIZE), :],
                dst_ref=land.at[half, me],
                send_sem=fwd_send.at[half, step],
                recv_sem=fwd_recv.at[half, step],
                device_id={"ctx": peer},
                device_id_type=MESH,
            )
            copy.start()
            fwd_copies[half].append(copy)
        land[half, me] = gct[
            pl.ds(pl.multiple_of(half * half_ch + me * GSIZE, GSIZE), GSIZE), :
        ]

    loads[4].wait()
    for block in range(blocks):
        gq[block, 0:rows] = go_v[:, columns(block)].astype(jnp.float32) * sc_v[
            :, columns(block)
        ].astype(jnp.float32)
    gq_copy = pltpu.make_async_remote_copy(
        src_ref=gq.at[:, pl.ds(0, HALO), :],
        dst_ref=gq.at[:, pl.ds(rows, HALO), :],
        send_sem=halo_send.at[5],
        recv_sem=halo_recv.at[5],
        device_id={"ctx": down},
        device_id_type=MESH,
    )
    gq_copy.start()
    loads[2].wait()
    loads[3].wait()
    for copy in halo_copies[1:]:
        copy.wait()
    for block in range(blocks):
        kfeat[block] = feature(1, k_v, block, 0, rows + HALO)
        vfeat[block] = feature(2, v_v, block, 1, rows + HALO)

    bwd_copies = [[], []]
    row_blocks = tokens // BLOCK
    for half in range(2):
        xrows[row_blocks * GSIZE :] = jnp.zeros(
            (xrows.shape[0] - row_blocks * GSIZE, BLOCK), jnp.bfloat16
        )
        for copy in fwd_copies[half]:
            copy.wait()
        for source in range(n_ctx):
            for tile in range(tiles):
                place, side = divmod(source * tiles + tile, 2)
                xrows[GSIZE * place : GSIZE * (place + 1), columns(side)] = land[
                    half, source, :, columns(tile)
                ]
        for part in range(3):
            amount = row_blocks * GSIZE - part * LANE
            left = jnp.concatenate(
                [xrows[GSIZE * d : GSIZE * d + amount, :] for d in range(8 * part, 8 * part + 8)],
                axis=1,
            )
            right = jnp.concatenate(
                [
                    toep[half, :, LANE * (lag_tiles - e) : LANE * (lag_tiles - e + 2)]
                    for e in range(16 * part, 16 * part + 16)
                ],
                axis=0,
            )
            product = jnp.dot(left, right, preferred_element_type=jnp.float32)
            if part == 0:
                acc[...] = product
            else:
                acc[0:amount] += product
        for target in range(n_ctx):
            for tile in range(tiles + 1):
                place, side = divmod(target * tiles + tile, 2)
                if place < row_blocks:
                    value = acc[GSIZE * place : GSIZE * (place + 1), columns(side)]
                else:
                    value = jnp.zeros((GSIZE, LANE), jnp.float32)
                back[half, target, :, columns(tile)] = value.astype(jnp.bfloat16)
        spot = pl.ds(pl.multiple_of(half * half_ch + me * GSIZE, GSIZE), GSIZE)
        for step in range(1, n_ctx):
            peer = lax.rem(me + step, n_ctx)
            copy = pltpu.make_async_remote_copy(
                src_ref=back.at[half, peer],
                dst_ref=mix.at[spot, :],
                send_sem=bwd_send.at[half, step],
                recv_sem=bwd_recv.at[half, step],
                device_id={"ctx": peer},
                device_id_type=MESH,
            )
            copy.start()
            bwd_copies[half].append(copy)
        mix[spot, :] = back[half, me]

    gq_copy.wait()
    for block in range(blocks):
        gq[block, rows : rows + HALO] = jnp.where(
            me == n_ctx - 1, 0.0, gq[block, rows : rows + HALO]
        )
        oq_v[:, columns(block)] = spread(taps, 0, gq.at[block], block, rows)
    for copy in bwd_copies[0]:
        copy.wait()
    for block in range(blocks // 2):
        finish(taps, mix, kfeat, vfeat, prod, ok_v, ov_v, block, block, rows)
    for copy in bwd_copies[1]:
        copy.wait()


def spread(taps, stream, source, block, rows):
    where = slice(LANE * block, LANE * (block + 1))
    total = taps[stream, 0:1, where] * source[0:rows]
    for offset in range(1, TAPS):
        total = total + taps[stream, offset : offset + 1, where] * source[offset : offset + rows]
    return total.astype(jnp.bfloat16)


def finish(taps, mix, kfeat, vfeat, prod, ok_v, ov_v, block, place, rows):
    channel = slice(LANE * block, LANE * (block + 1))
    target = slice(LANE * place, LANE * (place + 1))
    here = mix[channel, 0:rows].astype(jnp.float32).T
    there = mix[channel, rows : rows + LANE].astype(jnp.float32).T
    whole = jnp.concatenate([here, there[0:HALO]], axis=0)
    prod[0] = whole * vfeat[block]
    prod[1] = whole * kfeat[block]
    ok_v[:, target] = spread(taps, 1, prod.at[0], block, rows)
    ov_v[:, target] = spread(taps, 2, prod.at[1], block, rows)


def last_kernel(taps, oq_v, ok_v, ov_v, mix, kfeat, vfeat, oq, ok, ov, prod, ok_rest, ov_rest, sem):
    rows, channels = oq_v.shape
    half_ch = channels // 2
    blocks = channels // LANE
    copies = [
        pltpu.make_async_copy(oq_v, oq, sem.at[0]),
        pltpu.make_async_copy(ok_v, ok.at[:, pl.ds(0, half_ch)], sem.at[1]),
        pltpu.make_async_copy(ov_v, ov.at[:, pl.ds(0, half_ch)], sem.at[2]),
    ]
    for copy in copies:
        copy.start()
    for index, block in enumerate(range(blocks // 2, blocks)):
        finish(taps, mix, kfeat, vfeat, prod, ok_rest, ov_rest, block, index, rows)
        for which, (src, dst) in enumerate(((ok_rest, ok), (ov_rest, ov))):
            copy = pltpu.make_async_copy(
                src.at[:, pl.ds(LANE * index, LANE)],
                dst.at[:, pl.ds(LANE * block, LANE)],
                sem.at[3 + 2 * index + which],
            )
            copy.start()
            copies.append(copy)
    for copy in copies:
        copy.wait()


def body(n_ctx, n_tp, query_proj, key_proj, value_proj, saved_conv, grad_out, filters, featurizer):
    rows, channels = query_proj.shape
    tokens = filters.shape[1]
    blocks = channels // LANE
    bf16, f32 = jnp.bfloat16, jnp.float32
    dma = pltpu.SemaphoreType.DMA
    hbm = pl.BlockSpec(memory_space=pl.ANY)
    stream = pltpu.VMEM((rows, channels), bf16)
    conv_rows = tokens // BLOCK * GSIZE
    vmem = pl.BlockSpec(memory_space=pltpu.VMEM)
    between = [
        pltpu.VMEM(featurizer.shape, f32),
        pltpu.VMEM((rows, channels), bf16),
        pltpu.VMEM((rows, channels // 2), bf16),
        pltpu.VMEM((rows, channels // 2), bf16),
        pltpu.VMEM((channels, rows + LANE), bf16),
        pltpu.VMEM((blocks, rows + HALO, LANE), f32),
        pltpu.VMEM((blocks, rows + HALO, LANE), f32),
    ]
    first = pl.pallas_call(
        lambda *refs: kernel(n_ctx, n_tp, *refs),
        out_shape=between,
        in_specs=[hbm] * 7,
        out_specs=[vmem] * 7,
        scratch_shapes=[
            stream,
            stream,
            stream,
            stream,
            stream,
            pltpu.VMEM(filters.shape, bf16),
            pltpu.VMEM((3, HALO, channels), bf16),
            pltpu.VMEM((2, HALO, channels), bf16),
            pltpu.VMEM((rows + 2 * HALO, LANE), f32),
            pltpu.VMEM((blocks, rows, LANE), f32),
            pltpu.VMEM((blocks, rows + HALO, LANE), f32),
            pltpu.VMEM((2, LANE, tokens + 2 * LANE), bf16),
            pltpu.VMEM((channels, rows), bf16),
            pltpu.VMEM((2, n_ctx, GSIZE, rows), bf16),
            pltpu.VMEM((conv_rows + LANE, BLOCK), bf16),
            pltpu.VMEM((conv_rows, BLOCK), f32),
            pltpu.VMEM((2, n_ctx, GSIZE, rows + LANE), bf16),
            pltpu.VMEM((2, rows + HALO, LANE), f32),
            dma((7,)),
            dma((2, n_tp)),
            dma((2, n_tp)),
            dma((6,)),
            dma((6,)),
            dma((2, n_ctx)),
            dma((2, n_ctx)),
            dma((2, n_ctx)),
            dma((2, n_ctx)),
        ],
        compiler_params=pltpu.CompilerParams(
            collective_id=0, has_side_effects=True, vmem_limit_bytes=64_000_000
        ),
    )
    results = first(query_proj, key_proj, value_proj, saved_conv, grad_out, filters, featurizer)
    last = pl.pallas_call(
        last_kernel,
        out_shape=[jax.ShapeDtypeStruct((rows, channels), bf16)] * 3,
        in_specs=[vmem] * 7,
        out_specs=[hbm] * 3,
        scratch_shapes=[
            pltpu.VMEM((2, rows + HALO, LANE), f32),
            pltpu.VMEM((rows, channels // 2), bf16),
            pltpu.VMEM((rows, channels // 2), bf16),
            dma((3 + blocks,)),
        ],
        compiler_params=pltpu.CompilerParams(vmem_limit_bytes=16 << 20),
    )
    return tuple(last(*results))


def solution(mesh):
    n_ctx, n_tp = mesh.shape["ctx"], mesh.shape["tp"]
    return jax.shard_map(
        lambda *args: body(n_ctx, n_tp, *args),
        mesh=mesh,
        in_specs=(
            P("ctx", "tp"),
            P("ctx", "tp"),
            P("ctx", "tp"),
            P("ctx", "tp"),
            P(("ctx", "tp"), None),
            P("tp", None),
            P(None, None, "tp"),
        ),
        out_specs=(P("ctx", "tp"), P("ctx", "tp"), P("ctx", "tp")),
        check_vma=False,
    )
```
